512 devices in a mesh: dp: 8 (over y, z_hi), seq: 64 (over x, z_lo, core).
Axes of the slice: x: 4, y: 4, z: 16 (z_hi: 2, z_lo: 8; z = z_hi * 8 + z_lo), core: 2. Of those that a mesh axis runs over, the one named last changes fastest.
Arguments:
- grad_out: bfloat16 [8, 2048, 8192], P('dp', None, 'seq'), may hold values from -6 to 6
- gate: bfloat16 [8, 2048, 8192], P('dp', None, 'seq'), may hold values from -6 to 6
- value: bfloat16 [8, 2048, 8192], P('dp', None, 'seq'), may hold values from -6 to 6
- filter_taps: bfloat16 [2048, 8192], P(None, 'seq'), may hold values from -2 to 2
Outputs:
- grad_gate: bfloat16 [8, 2048, 8192], P('dp', None, 'seq')
- grad_value: bfloat16 [8, 2048, 8192], P('dp', None, 'seq')
- grad_filter: float32 [2048, 8192], P('seq', 'dp')
The draws below stay inside these ranges and needn't reach their ends.
All inputs are finite; a program needn't handle non-finite values.
Results may differ from the reference program's by a relative error of at most 0.017.
Values may be sent and summed in bfloat16 or wider, within the bound.
A program may use at most 128 MiB of HBM per device.

```python
import math
import jax
import jax.numpy as jnp
from jax import lax

CH = 2048
LEN = 8192
BATCH = 8


def draw_filter_taps(key, part):
    key_reach = jax.random.fold_in(key, 11)
    key_taps = jax.random.fold_in(key, 12)
    lowest = 30.0
    highest = LEN * 2.0
    fraction = jax.random.uniform(key_reach, (CH, 1), jnp.float32)
    reach = lowest * jnp.exp(fraction * jnp.log(highest / lowest))
    taps = jnp.clip(jax.random.normal(key_taps, (CH, LEN), jnp.float32), -6.0, 6.0)
    places = lax.broadcasted_iota(jnp.float32, (CH, LEN), 1)
    return (taps * jnp.sqrt(2.0 / reach) * jnp.exp(-places / reach)).astype(jnp.bfloat16)


def shard_levels(own_key, extent, cuts, smallest, high):
    level, own = 1.0, jax.random.fold_in(own_key, 6)
    for dim, shards_of in cuts:
        heights = jnp.exp(jax.random.uniform(jax.random.fold_in(own, dim), (shards_of,), jnp.float32, smallest / len(cuts), high / len(cuts)))
        level = level * jnp.repeat(heights, extent[dim] // shards_of).reshape([-1 if axis == dim else 1 for axis in range(len(extent))])
    return level


def centred(stream_key, shape, spread, bound, cuts=(), kind=jnp.bfloat16):
    level = shard_levels(stream_key, shape, cuts, -0.22, 0.18) if cuts else 1.0
    drawn = jax.random.normal(stream_key, shape, jnp.float32) * spread * level
    return jnp.minimum(jnp.maximum(drawn, -bound), bound).astype(kind)


def setup_inputs(seed: int = 0) -> dict:
    streams_of = jax.random.split(jax.random.key(seed), 5)
    return {
        "grad_out": centred(streams_of[0], (BATCH, CH, LEN), 1.0, 6.0, ((0, 8), (2, 64))),
        "gate": centred(streams_of[1], (BATCH, CH, LEN), 1.0, 6.0, ((0, 8), (2, 64))),
        "value": centred(streams_of[2], (BATCH, CH, LEN), 1.0, 6.0, ((0, 8), (2, 64))),
        "filter_taps": draw_filter_taps(jax.random.fold_in(streams_of[4], 71), 0),
    }


def per_block(pieces):
    grad_block, gate_block, value_block, filter_block = pieces
    size_n = 2 * LEN
    gated = (grad_block.astype(jnp.float32) * gate_block.astype(jnp.float32)).astype(jnp.bfloat16)
    gated = lax.optimization_barrier(gated).astype(jnp.float32)
    spec_gated = jnp.fft.rfft(gated, n=size_n, axis=-1)
    spec_value = jnp.fft.rfft(value_block.astype(jnp.float32), n=size_n, axis=-1)
    spec_filter = jnp.fft.rfft(filter_block.astype(jnp.float32), n=size_n, axis=-1)[None]
    conv = jnp.fft.irfft(spec_filter * spec_value, n=size_n, axis=-1)[..., :LEN].astype(jnp.bfloat16)
    conv = lax.optimization_barrier(conv)
    grad_gate = (grad_block.astype(jnp.float32) * conv.astype(jnp.float32)).astype(jnp.bfloat16)
    grad_value = jnp.fft.irfft(jnp.conj(spec_filter) * spec_gated, n=size_n, axis=-1)[..., :LEN].astype(jnp.bfloat16)
    cross = jnp.fft.irfft(jnp.conj(spec_value) * spec_gated, n=size_n, axis=-1)[..., :LEN]
    factor = 1.0 / (BATCH * math.sqrt(LEN))
    grad_filter = (lax.optimization_barrier(jnp.sum(cross, axis=0)) * factor).astype(jnp.float32)
    return (grad_gate, grad_value, grad_filter)

def reference(grad_out, gate, value, filter_taps):
    lanes = 128
    count = CH // lanes

    def split_rows(array):
        return array.reshape(BATCH, count, lanes, LEN).transpose(1, 0, 2, 3)
    pieces = (split_rows(grad_out), split_rows(gate), split_rows(value), filter_taps.reshape(count, lanes, LEN))
    grad_gate, grad_value, grad_filter = lax.map(per_block, pieces)
    grad_gate = grad_gate.transpose(1, 0, 2, 3).reshape(BATCH, CH, LEN)
    grad_value = grad_value.transpose(1, 0, 2, 3).reshape(BATCH, CH, LEN)
    return (grad_gate, grad_value, grad_filter.reshape(CH, LEN))
```

```python
import functools
import math

import jax
import jax.numpy as jnp
import numpy as np
from jax import lax
from jax.experimental import pallas as pl
from jax.experimental.pallas import tpu as pltpu
from jax.sharding import PartitionSpec as P

MESH = pl.DeviceIdType.MESH
GROUP = 16


def make_tables(blocks, width, offset=0.25):
    total = blocks * width
    source = np.arange(blocks)
    lane = np.arange(width)
    start_angle = 2 * np.pi * ((source[:, None] + offset) * source[None, :] % blocks) / blocks
    start = np.concatenate([np.cos(start_angle), -np.sin(start_angle)], 0)
    twist = 2 * np.pi * ((source[:, None] + offset) * lane[None, :] % total) / total
    inner = 2 * np.pi * (lane[:, None] * lane[None, :] % width) / width
    cos, sin = np.cos(inner), np.sin(inner)
    forward = np.block([[cos, -sin], [sin, cos]])
    backward = np.block([[cos, sin], [-sin, cos]])
    finish = np.concatenate([np.cos(start_angle.T), -np.sin(start_angle.T)], 1) / total
    narrow = [jnp.asarray(table, jnp.bfloat16) for table in (start, forward, backward, finish)]
    wide = [jnp.asarray(table, jnp.float32) for table in (np.cos(twist), np.sin(twist))]
    return (*narrow, *wide)


def dot(left, right):
    return jnp.dot(left, right, preferred_element_type=jnp.float32)


def forward_spectrum(signal, spectrum, mixed, tables):
    start, forward, _, _, twist_cos, twist_sin = tables
    blocks, chans, width = signal.shape

    def body(step, carry):
        first = pl.multiple_of(step * GROUP, GROUP)
        columns = signal[:, pl.ds(first, GROUP), :].astype(jnp.float32)
        columns = jnp.swapaxes(columns, 0, 1).astype(jnp.bfloat16)
        cos, sin = twist_cos[...], twist_sin[...]
        for chan in range(GROUP):
            stage = dot(start[...], columns[chan])
            real, imag = stage[:blocks], stage[blocks:]
            rows = slice(chan * blocks, (chan + 1) * blocks)
            mixed[rows, :width] = (real * cos + imag * sin).astype(jnp.bfloat16)
            mixed[rows, width:] = (imag * cos - real * sin).astype(jnp.bfloat16)
        spectrum[pl.ds(first * blocks, GROUP * blocks), :] = dot(mixed[...], forward[...])
        return carry

    lax.fori_loop(0, chans // GROUP, body, 0)


def inverse_product(left, right, conjugate, result, mixed, partial, columns, tables):
    _, _, backward, finish, twist_cos, twist_sin = tables
    blocks, chans, width = result.shape

    def body(step, carry):
        first = pl.multiple_of(step * GROUP, GROUP)
        rows = pl.ds(first * blocks, GROUP * blocks)
        left_real, left_imag = left[rows, :width], left[rows, width:]
        right_real, right_imag = right[rows, :width], right[rows, width:]
        if conjugate:
            real = left_real * right_real + left_imag * right_imag
            imag = left_real * right_imag - left_imag * right_real
        else:
            real = left_real * right_real - left_imag * right_imag
            imag = left_real * right_imag + left_imag * right_real
        mixed[:, :width] = real.astype(jnp.bfloat16)
        mixed[:, width:] = imag.astype(jnp.bfloat16)
        partial[...] = dot(mixed[...], backward[...])
        cos, sin = twist_cos[...], twist_sin[...]
        for chan in range(GROUP):
            here = slice(chan * blocks, (chan + 1) * blocks)
            real, imag = partial[here, :width], partial[here, width:]
            turned = jnp.concatenate([real * cos - imag * sin, real * sin + imag * cos], 0)
            columns[chan] = dot(finish[...], turned.astype(jnp.bfloat16))
        result[:, pl.ds(first, GROUP), :] = jnp.swapaxes(columns[...], 0, 1).astype(result.dtype)
        return carry

    lax.fori_loop(0, chans // GROUP, body, 0)


def scatter(source, target, send_sem, recv_sem, me, nseq):
    def body(shift, carry):
        peer = lax.rem(me + shift, nseq)
        pltpu.make_async_remote_copy(
            src_ref=source.at[peer],
            dst_ref=target.at[me],
            send_sem=send_sem,
            recv_sem=recv_sem,
            device_id={"seq": peer},
            device_id_type=MESH,
        ).start()
        return carry

    lax.fori_loop(1, nseq, body, 0)
    pltpu.make_async_copy(source.at[me], target.at[me], recv_sem).start()


def take(ref, sem):
    pltpu.make_async_copy(ref, ref, sem).wait()


def kernel(
    factor,
    value,
    gated,
    taps,
    start,
    forward,
    backward,
    finish,
    twist_cos,
    twist_sin,
    conv_back,
    grad_back,
    filter_grad,
    value_cols,
    gated_cols,
    taps_cols,
    conv_send,
    grad_send,
    cross,
    y_recv,
    z_send,
    z_recv,
    spec_value,
    spec_gated,
    spec_taps,
    mixed,
    partial,
    columns,
    send_sem,
    recv_sem,
):
    tables = (start, forward, backward, finish, twist_cos, twist_sin)
    nseq = value.shape[0]
    me = lax.axis_index("seq")
    dp = lax.axis_index("dp")
    plane, half = dp // 2, lax.rem(dp, 2)
    depth = lax.rem(me // 2, 4)
    other_half = plane * 2 + 1 - half
    flat_taps = taps_cols

    barrier = pltpu.get_barrier_semaphore()

    def greet(shift, carry):
        pl.semaphore_signal(
            barrier, inc=1, device_id={"seq": lax.rem(me + shift, nseq)}, device_id_type=MESH
        )
        return carry

    lax.fori_loop(1, nseq, greet, 0)
    for shift in range(1, 4):
        neighbour = lax.rem(plane + shift, 4) * 2 + half
        pl.semaphore_signal(barrier, inc=1, device_id={"dp": neighbour}, device_id_type=MESH)
    pl.semaphore_signal(barrier, inc=1, device_id={"dp": other_half}, device_id_type=MESH)
    pl.semaphore_wait(barrier, nseq + 3)

    def quarter(depth_here):
        return lax.rem(plane + 4 - depth_here, 4)

    mine = quarter(depth)

    def send_taps(step, carry):
        peer = (step // 2) * 8 + mine * 2 + lax.rem(step, 2)

        @pl.when(peer != me)
        def _():
            pltpu.make_async_remote_copy(
                src_ref=taps.at[peer // 8, lax.rem(peer // 2, 4), lax.rem(peer, 2)],
                dst_ref=taps_cols.at[me // 8, depth, lax.rem(me, 2)],
                send_sem=send_sem.at[0],
                recv_sem=recv_sem.at[0],
                device_id={"seq": peer},
                device_id_type=MESH,
            ).start()

        @pl.when(peer == me)
        def _():
            pltpu.make_async_copy(
                taps.at[me // 8, depth, lax.rem(me, 2)],
                taps_cols.at[me // 8, depth, lax.rem(me, 2)],
                recv_sem.at[0],
            ).start()

        return carry

    lax.fori_loop(0, nseq // 4, send_taps, 0)
    scatter(value, value_cols, send_sem.at[1], recv_sem.at[1], me, nseq)
    scatter(gated, gated_cols, send_sem.at[2], recv_sem.at[2], me, nseq)

    take(taps_cols.at[:, mine], recv_sem.at[0])
    for shift in range(1, 4):
        neighbour = lax.rem(plane + shift, 4) * 2 + half
        pltpu.make_async_remote_copy(
            src_ref=taps_cols.at[:, mine],
            dst_ref=taps_cols.at[:, mine],
            send_sem=send_sem.at[3],
            recv_sem=recv_sem.at[3],
            device_id={"dp": neighbour},
            device_id_type=MESH,
        ).start()
    take(taps_cols.at[:, pl.ds(0, 3)], recv_sem.at[3])
    taps_view = taps_cols.reshape(value.shape)
    forward_spectrum(taps_view, spec_taps, mixed, tables)

    take(value_cols, recv_sem.at[1])
    forward_spectrum(value_cols, spec_value, mixed, tables)
    inverse_product(spec_taps, spec_value, False, conv_send, mixed, partial, columns, tables)
    scatter(conv_send, conv_back, send_sem.at[4], recv_sem.at[4], me, nseq)

    take(gated_cols, recv_sem.at[2])
    forward_spectrum(gated_cols, spec_gated, mixed, tables)
    inverse_product(spec_taps, spec_gated, True, grad_send, mixed, partial, columns, tables)
    scatter(grad_send, grad_back, send_sem.at[5], recv_sem.at[5], me, nseq)

    inverse_product(spec_value, spec_gated, True, cross, mixed, partial, columns, tables)
    for shift in range(1, 4):
        other = lax.rem(plane + shift, 4)
        pltpu.make_async_remote_copy(
            src_ref=cross.at[pl.ds(other * 16, 16)],
            dst_ref=y_recv.at[shift - 1],
            send_sem=send_sem.at[6],
            recv_sem=recv_sem.at[6],
            device_id={"dp": other * 2 + half},
            device_id_type=MESH,
        ).start()
    take(y_recv, recv_sem.at[6])
    gone = plane * 16 + 8 * (1 - half)
    away = pl.ds(8 * (1 - half), 8)
    z_send[...] = (
        cross[pl.ds(gone, 8)] + y_recv[0, away] + y_recv[1, away] + y_recv[2, away]
    ).astype(z_send.dtype)
    swap = pltpu.make_async_remote_copy(
        src_ref=z_send,
        dst_ref=z_recv,
        send_sem=send_sem.at[7],
        recv_sem=recv_sem.at[7],
        device_id={"dp": other_half},
        device_id_type=MESH,
    )
    swap.start()
    kept = plane * 16 + 8 * half
    stay = pl.ds(8 * half, 8)
    total = cross[pl.ds(kept, 8)] + y_recv[0, stay] + y_recv[1, stay] + y_recv[2, stay]
    swap.wait()
    width = value.shape[2]
    total = (total + z_recv[...].astype(jnp.float32)) * factor
    for block in range(8):
        filter_grad[:, block * width : (block + 1) * width] = total[block]

    take(conv_back, recv_sem.at[4])
    take(grad_back, recv_sem.at[5])
    for index, ref in ((1, value), (2, gated), (4, conv_send), (5, grad_send)):
        take(ref.at[pl.ds(0, nseq - 1)], send_sem.at[index])
    take(taps_cols.at[:, pl.ds(0, 3)], send_sem.at[3])
    take(y_recv, send_sem.at[6])

    @pl.when(mine == depth)
    def _():
        take(value.at[pl.ds(0, nseq // 4 - 1)], send_sem.at[0])

    @pl.when(mine != depth)
    def _():
        take(value.at[pl.ds(0, nseq // 4)], send_sem.at[0])


def run_kernel(value, gated, taps, factor):
    nseq, group, width = value.shape
    narrow, wide = jnp.bfloat16, jnp.float32
    blocks = (nseq, group, width)
    shapes = [
        jax.ShapeDtypeStruct(blocks, narrow),
        jax.ShapeDtypeStruct(blocks, narrow),
        jax.ShapeDtypeStruct((group, nseq * width // 8), wide),
    ]
    tables = make_tables(nseq, width)
    quarters = (nseq // 8, 4, 2, group, width)
    spec = (group * nseq, 2 * width)
    part = (GROUP * nseq, 2 * width)
    place = pl.BlockSpec(memory_space=pltpu.VMEM)
    return pl.pallas_call(
        functools.partial(kernel, factor),
        out_shape=shapes,
        in_specs=[place] * (3 + len(tables)),
        out_specs=[place] * 3,
        scratch_shapes=[
            pltpu.VMEM(blocks, narrow),
            pltpu.VMEM(blocks, narrow),
            pltpu.VMEM(quarters, narrow),
            pltpu.VMEM(blocks, narrow),
            pltpu.VMEM(blocks, narrow),
            pltpu.VMEM(blocks, wide),
            pltpu.VMEM((3, 16, group, width), wide),
            pltpu.VMEM((8, group, width), narrow),
            pltpu.VMEM((8, group, width), narrow),
            pltpu.VMEM(spec, wide),
            pltpu.VMEM(spec, wide),
            pltpu.VMEM(spec, wide),
            pltpu.VMEM(part, narrow),
            pltpu.VMEM(part, wide),
            pltpu.VMEM((GROUP, nseq, width), wide),
            pltpu.SemaphoreType.DMA((8,)),
            pltpu.SemaphoreType.DMA((8,)),
        ],
        compiler_params=pltpu.CompilerParams(
            collective_id=0, has_side_effects=True, vmem_limit_bytes=48 * 2**20
        ),
    )(value, gated, taps.reshape(quarters), *tables)


def on_device(grad_out, gate, value, filter_taps):
    nseq = lax.axis_size("seq")
    ndp = lax.axis_size("dp")
    chans, width = grad_out.shape[1:]
    blocks = (nseq, chans // nseq, width)
    gated = (grad_out[0].astype(jnp.float32) * gate[0].astype(jnp.float32)).astype(jnp.bfloat16)
    factor = 1.0 / (ndp * math.sqrt(nseq * width))
    conv, grad_value, grad_filter = run_kernel(
        value[0].reshape(blocks), gated.reshape(blocks), filter_taps.reshape(blocks), factor
    )
    conv = conv.reshape(chans, width)
    grad_gate = (grad_out[0].astype(jnp.float32) * conv.astype(jnp.float32)).astype(jnp.bfloat16)
    return (grad_gate[None], grad_value.reshape(1, chans, width), grad_filter)


def solution(mesh):
    return jax.shard_map(
        on_device,
        mesh=mesh,
        in_specs=(P("dp", None, "seq"), P("dp", None, "seq"), P("dp", None, "seq"), P(None, "seq")),
        out_specs=(P("dp", None, "seq"), P("dp", None, "seq"), P("seq", "dp")),
        check_vma=False,
    )
```

```python
import functools
import math

import jax
import jax.numpy as jnp
import numpy as np
from jax import lax
from jax.experimental import pallas as pl
from jax.experimental.pallas import tpu as pltpu
from jax.sharding import PartitionSpec as P

MESH = pl.DeviceIdType.MESH
GROUP = 16
EARLY = 40
FIRST = 32


def make_tables(blocks, width, offset=0.25):
    total = blocks * width
    source = np.arange(blocks)
    lane = np.arange(width)
    start_angle = 2 * np.pi * ((source[:, None] + offset) * source[None, :] % blocks) / blocks
    start = np.concatenate([np.cos(start_angle), -np.sin(start_angle)], 0)
    twist = 2 * np.pi * ((source[:, None] + offset) * lane[None, :] % total) / total
    inner = 2 * np.pi * (lane[:, None] * lane[None, :] % width) / width
    cos, sin = np.cos(inner), np.sin(inner)
    forward = np.block([[cos, -sin], [sin, cos]])
    backward = np.block([[cos, sin], [-sin, cos]])
    finish = np.concatenate([np.cos(start_angle.T), -np.sin(start_angle.T)], 1) / total
    narrow = [jnp.asarray(table, jnp.bfloat16) for table in (start, forward, backward, finish)]
    wide = [jnp.asarray(table, jnp.float32) for table in (np.cos(twist), np.sin(twist))]
    return (*narrow, *wide)


def dot(left, right):
    return jnp.dot(left, right, preferred_element_type=jnp.float32)


def forward_spectrum(signal, spectrum, mixed, tables):
    start, forward, _, _, twist_cos, twist_sin = tables
    blocks, chans, width = signal.shape

    def body(step, carry):
        first = pl.multiple_of(step * GROUP, GROUP)
        columns = signal[:, pl.ds(first, GROUP), :].astype(jnp.float32)
        columns = jnp.swapaxes(columns, 0, 1).astype(jnp.bfloat16)
        cos, sin = twist_cos[...], twist_sin[...]
        for chan in range(GROUP):
            stage = dot(start[...], columns[chan])
            real, imag = stage[:blocks], stage[blocks:]
            rows = slice(chan * blocks, (chan + 1) * blocks)
            mixed[rows, :width] = (real * cos + imag * sin).astype(jnp.bfloat16)
            mixed[rows, width:] = (imag * cos - real * sin).astype(jnp.bfloat16)
        spectrum[pl.ds(first * blocks, GROUP * blocks), :] = dot(mixed[...], forward[...])
        return carry

    lax.fori_loop(0, chans // GROUP, body, 0)


def inverse_product(left, right, conjugate, result, mixed, partial, columns, tables):
    _, _, backward, finish, twist_cos, twist_sin = tables
    blocks, chans, width = result.shape

    def body(step, carry):
        first = pl.multiple_of(step * GROUP, GROUP)
        rows = pl.ds(first * blocks, GROUP * blocks)
        left_real, left_imag = left[rows, :width], left[rows, width:]
        right_real, right_imag = right[rows, :width], right[rows, width:]
        if conjugate:
            real = left_real * right_real + left_imag * right_imag
            imag = left_real * right_imag - left_imag * right_real
        else:
            real = left_real * right_real - left_imag * right_imag
            imag = left_real * right_imag + left_imag * right_real
        mixed[:, :width] = real.astype(jnp.bfloat16)
        mixed[:, width:] = imag.astype(jnp.bfloat16)
        partial[...] = dot(mixed[...], backward[...])
        cos, sin = twist_cos[...], twist_sin[...]
        for chan in range(GROUP):
            here = slice(chan * blocks, (chan + 1) * blocks)
            real, imag = partial[here, :width], partial[here, width:]
            turned = jnp.concatenate([real * cos - imag * sin, real * sin + imag * cos], 0)
            columns[chan] = dot(finish[...], turned.astype(jnp.bfloat16))
        result[:, pl.ds(first, GROUP), :] = jnp.swapaxes(columns[...], 0, 1).astype(result.dtype)
        return carry

    lax.fori_loop(0, chans // GROUP, body, 0)


def scatter(source, target, send_sem, recv_sem, me, nseq, first=0, last=None):
    def body(shift, carry):
        peer = lax.rem(me + shift, nseq)
        pltpu.make_async_remote_copy(
            src_ref=source.at[peer],
            dst_ref=target.at[me],
            send_sem=send_sem,
            recv_sem=recv_sem,
            device_id={"seq": peer},
            device_id_type=MESH,
        ).start()
        return carry

    lax.fori_loop(max(first, 1), nseq if last is None else last, body, 0)
    if first == 0:
        pltpu.make_async_copy(source.at[me], target.at[me], recv_sem).start()


def take(ref, sem):
    pltpu.make_async_copy(ref, ref, sem).wait()


def times(left, right, result):
    def body(step, carry):
        rows = pl.ds(step * 8, 8)
        product = left[rows].astype(jnp.float32) * right[rows].astype(jnp.float32)
        result[rows] = product.astype(result.dtype)
        return carry

    lax.fori_loop(0, left.shape[0] // 8, body, 0)


def kernel(
    factor,
    grad_out,
    gate,
    value,
    taps,
    start,
    forward,
    backward,
    finish,
    twist_cos,
    twist_sin,
    grad_gate,
    grad_back,
    filter_grad,
    grad_held,
    gate_held,
    gated,
    value_cols,
    gated_cols,
    taps_cols,
    conv_send,
    conv_back,
    grad_send,
    cross,
    y_send,
    y_recv,
    z_send,
    z_recv,
    spec_value,
    spec_gated,
    spec_taps,
    mixed,
    partial,
    columns,
    gate_out,
    filter_out,
    send_sem,
    recv_sem,
    load_sem,
):
    tables = (start, forward, backward, finish, twist_cos, twist_sin)
    nseq = value.shape[0]
    me = lax.axis_index("seq")
    dp = lax.axis_index("dp")
    plane, half = dp // 2, lax.rem(dp, 2)
    depth = lax.rem(me // 2, 4)
    upper = lax.rem(me // 8, 2)
    other_half = plane * 2 + 1 - half
    mine = lax.rem(plane + 4 - depth, 4)

    def taps_peer(step):
        far = lax.rem(step // 2, 2)
        peer = (step // 2) * 8 + mine * 2 + lax.rem(step, 2)
        return peer, plane * 2 + lax.rem(half + upper + far, 2)

    barrier = pltpu.get_barrier_semaphore()

    def greet(shift, carry):
        pl.semaphore_signal(
            barrier, inc=1, device_id={"seq": lax.rem(me + shift, nseq)}, device_id_type=MESH
        )
        return carry

    def greet_taps(step, carry):
        peer, row = taps_peer(step)

        @pl.when(row != dp)
        def _():
            pl.semaphore_signal(
                barrier, inc=1, device_id={"dp": row, "seq": peer}, device_id_type=MESH
            )

        return carry

    lax.fori_loop(1, nseq, greet, 0)
    lax.fori_loop(0, nseq // 4, greet_taps, 0)
    for shift in range(1, 4):
        neighbour = lax.rem(plane + shift, 4) * 2 + half
        pl.semaphore_signal(barrier, inc=1, device_id={"dp": neighbour}, device_id_type=MESH)
    pl.semaphore_signal(barrier, inc=1, device_id={"dp": other_half}, device_id_type=MESH)

    loads = [
        pltpu.make_async_copy(grad_out, grad_held, load_sem.at[0]),
        pltpu.make_async_copy(gate, gate_held, load_sem.at[1]),
    ]
    for load in loads:
        load.start()
    for load in loads:
        load.wait()
    times(grad_held, gate_held, gated)
    pl.semaphore_wait(barrier, nseq + 3 + nseq // 8)

    scatter(value, value_cols, send_sem.at[1], recv_sem.at[1], me, nseq, 0, EARLY)
    scatter(value, value_cols, send_sem.at[1], recv_sem.at[8], me, nseq, EARLY)

    def send_taps(step, carry):
        peer, row = taps_peer(step)
        itself = jnp.logical_and(peer == me, row == dp)

        @pl.when(jnp.logical_not(itself))
        def _():
            pltpu.make_async_remote_copy(
                src_ref=taps.at[peer // 8, lax.rem(peer // 2, 4), lax.rem(peer, 2)],
                dst_ref=taps_cols.at[me // 8, depth, lax.rem(me, 2)],
                send_sem=send_sem.at[0],
                recv_sem=recv_sem.at[0],
                device_id={"dp": row, "seq": peer},
                device_id_type=MESH,
            ).start()

        @pl.when(itself)
        def _():
            pltpu.make_async_copy(
                taps.at[me // 8, depth, lax.rem(me, 2)],
                taps_cols.at[me // 8, depth, lax.rem(me, 2)],
                recv_sem.at[0],
            ).start()

        return carry

    lax.fori_loop(0, nseq // 4, send_taps, 0)
    take(value_cols.at[pl.ds(0, EARLY)], recv_sem.at[1])
    scatter(gated, gated_cols, send_sem.at[2], recv_sem.at[2], me, nseq)

    take(taps_cols.at[:, mine], recv_sem.at[0])
    for shift in range(1, 4):
        neighbour = lax.rem(plane + shift, 4) * 2 + half
        pltpu.make_async_remote_copy(
            src_ref=taps_cols.at[:, mine],
            dst_ref=taps_cols.at[:, mine],
            send_sem=send_sem.at[3],
            recv_sem=recv_sem.at[3],
            device_id={"dp": neighbour},
            device_id_type=MESH,
        ).start()
    take(taps_cols.at[:, pl.ds(0, 3)], recv_sem.at[3])
    forward_spectrum(taps_cols.reshape(value.shape), spec_taps, mixed, tables)

    take(value_cols.at[pl.ds(EARLY, nseq - EARLY)], recv_sem.at[8])
    forward_spectrum(value_cols, spec_value, mixed, tables)
    inverse_product(spec_taps, spec_value, False, conv_send, mixed, partial, columns, tables)
    scatter(conv_send, conv_back, send_sem.at[4], recv_sem.at[4], me, nseq, 0, FIRST)

    take(gated_cols, recv_sem.at[2])
    forward_spectrum(gated_cols, spec_gated, mixed, tables)
    inverse_product(spec_value, spec_gated, True, cross, mixed, partial, columns, tables)
    for shift in range(1, 4):
        other = lax.rem(plane + shift, 4)
        y_send[shift - 1] = cross[pl.ds(other * 16, 16)].astype(y_send.dtype)
    for shift in range(1, 4):
        other = lax.rem(plane + shift, 4)
        pltpu.make_async_remote_copy(
            src_ref=y_send.at[shift - 1],
            dst_ref=y_recv.at[shift - 1],
            send_sem=send_sem.at[6],
            recv_sem=recv_sem.at[6],
            device_id={"dp": other * 2 + half},
            device_id_type=MESH,
        ).start()
    scatter(conv_send, conv_back, send_sem.at[4], recv_sem.at[4], me, nseq, FIRST)
    inverse_product(spec_taps, spec_gated, True, grad_send, mixed, partial, columns, tables)
    scatter(grad_send, grad_back, send_sem.at[5], recv_sem.at[5], me, nseq, 0, FIRST)

    take(y_recv, recv_sem.at[6])

    def plane_sum(part):
        rows = pl.ds(8 * part, 8)
        terms = [y_recv[index, rows].astype(jnp.float32) for index in range(3)]
        return cross[pl.ds(plane * 16 + 8 * part, 8)] + terms[0] + terms[1] + terms[2]

    z_send[...] = plane_sum(1 - half).astype(z_send.dtype)
    swap = pltpu.make_async_remote_copy(
        src_ref=z_send,
        dst_ref=z_recv,
        send_sem=send_sem.at[7],
        recv_sem=recv_sem.at[7],
        device_id={"dp": other_half},
        device_id_type=MESH,
    )
    swap.start()
    scatter(grad_send, grad_back, send_sem.at[5], recv_sem.at[5], me, nseq, FIRST)

    take(conv_back, recv_sem.at[4])
    times(grad_held, conv_back, gate_out)
    gate_store = pltpu.make_async_copy(gate_out, grad_gate, load_sem.at[2])
    gate_store.start()

    total = plane_sum(half)
    swap.wait()
    width = value.shape[2]
    total = (total + z_recv[...].astype(jnp.float32)) * factor
    for block in range(8):
        filter_out[:, block * width : (block + 1) * width] = total[block]
    filter_store = pltpu.make_async_copy(filter_out, filter_grad, load_sem.at[3])
    filter_store.start()
    gate_store.wait()

    for index, ref in ((1, value_cols), (2, gated), (4, conv_send)):
        take(ref.at[pl.ds(0, nseq - 1)], send_sem.at[index])
    take(taps_cols.at[:, pl.ds(0, 3)], send_sem.at[3])
    take(y_recv, send_sem.at[6])
    itself_too = mine == depth

    @pl.when(itself_too)
    def _():
        take(value_cols.at[pl.ds(0, nseq // 4 - 1)], send_sem.at[0])

    @pl.when(jnp.logical_not(itself_too))
    def _():
        take(value_cols.at[pl.ds(0, nseq // 4)], send_sem.at[0])

    take(grad_send.at[pl.ds(0, nseq - 1)], send_sem.at[5])
    filter_store.wait()
    take(grad_back, recv_sem.at[5])


def flush(*refs):
    count = len(refs) // 3
    sources, targets, held = refs[:count], refs[count : 2 * count], refs[2 * count : 3 * count]
    loads, stores = [], []
    for index in range(count):
        rows = held[index].shape[0] // 4
        for step in range(4):
            part = pl.ds(step * rows, rows)
            sem = 4 * index + step
            loads.append(
                pltpu.make_async_copy(
                    sources[index].at[part], held[index].at[part], refs[-1].at[0, sem]
                )
            )
            stores.append(
                pltpu.make_async_copy(
                    held[index].at[part], targets[index].at[part], refs[-1].at[1, sem]
                )
            )
    for load in loads:
        load.start()
    for load, store in zip(loads, stores):
        load.wait()
        store.start()
    for store in stores:
        store.wait()


def run_kernel(grad_out, gate, value, taps, factor):
    nseq, group, width = value.shape
    narrow, wide = jnp.bfloat16, jnp.float32
    blocks = (nseq, group, width)
    shapes = [
        jax.ShapeDtypeStruct(blocks, narrow),
        jax.ShapeDtypeStruct(blocks, narrow),
        jax.ShapeDtypeStruct((group, nseq * width // 8), wide),
    ]
    tables = make_tables(nseq, width)
    quarters = (nseq // 8, 4, 2, group, width)
    spec = (group * nseq, 2 * width)
    part = (GROUP * nseq, 2 * width)
    place = pl.BlockSpec(memory_space=pltpu.VMEM)
    far = pl.BlockSpec(memory_space=pl.ANY)
    results = pl.pallas_call(
        functools.partial(kernel, factor),
        out_shape=shapes,
        in_specs=[far] * 4 + [place] * len(tables),
        out_specs=[far] * 3,
        scratch_shapes=[pltpu.VMEM(blocks, narrow) for _ in range(5)]
        + [pltpu.VMEM(quarters, narrow)]
        + [pltpu.VMEM(blocks, narrow) for _ in range(3)]
        + [
            pltpu.VMEM(blocks, wide),
            pltpu.VMEM((3, 16, group, width), narrow),
            pltpu.VMEM((3, 16, group, width), narrow),
            pltpu.VMEM((8, group, width), narrow),
            pltpu.VMEM((8, group, width), narrow),
            pltpu.VMEM(spec, wide),
            pltpu.VMEM(spec, wide),
            pltpu.VMEM(spec, wide),
            pltpu.VMEM(part, narrow),
            pltpu.VMEM(part, wide),
            pltpu.VMEM((GROUP, nseq, width), wide),
            pltpu.VMEM(blocks, narrow),
            pltpu.VMEM((group, nseq * width // 8), wide),
            pltpu.SemaphoreType.DMA((8,)),
            pltpu.SemaphoreType.DMA((9,)),
            pltpu.SemaphoreType.DMA((4,)),
        ],
        compiler_params=pltpu.CompilerParams(
            collective_id=0, has_side_effects=True, vmem_limit_bytes=60 * 2**20
        ),
    )(grad_out, gate, value, taps.reshape(quarters), *tables)
    return pl.pallas_call(
        flush,
        out_shape=shapes,
        in_specs=[far] * 3,
        out_specs=[far] * 3,
        scratch_shapes=[pltpu.VMEM(shape.shape, shape.dtype) for shape in shapes]
        + [pltpu.SemaphoreType.DMA((2, 12))],
        compiler_params=pltpu.CompilerParams(vmem_limit_bytes=60 * 2**20),
    )(*results)


def on_device(grad_out, gate, value, filter_taps):
    nseq = lax.axis_size("seq")
    ndp = lax.axis_size("dp")
    chans, width = grad_out.shape[1:]
    blocks = (nseq, chans // nseq, width)
    factor = 1.0 / (ndp * math.sqrt(nseq * width))
    grad_gate, grad_value, grad_filter = run_kernel(
        *(array.reshape(blocks) for array in (grad_out, gate, value, filter_taps)), factor
    )
    whole = (1, chans, width)
    return (grad_gate.reshape(whole), grad_value.reshape(whole), grad_filter)


def solution(mesh):
    return jax.shard_map(
        on_device,
        mesh=mesh,
        in_specs=(P("dp", None, "seq"), P("dp", None, "seq"), P("dp", None, "seq"), P(None, "seq")),
        out_specs=(P("dp", None, "seq"), P("dp", None, "seq"), P("seq", "dp")),
        check_vma=False,
    )
```

```python
import functools
import math

import jax
import jax.numpy as jnp
import numpy as np
from jax import lax
from jax.experimental import pallas as pl
from jax.experimental.pallas import tpu as pltpu
from jax.sharding import PartitionSpec as P

MESH = pl.DeviceIdType.MESH
GROUP = 16
EARLY = 40
FIRST = 46
HALF = 40


def make_tables(blocks, width, offset=0.25):
    total = blocks * width
    source = np.arange(blocks)
    lane = np.arange(width)
    start_angle = 2 * np.pi * ((source[:, None] + offset) * source[None, :] % blocks) / blocks
    start = np.concatenate([np.cos(start_angle), -np.sin(start_angle)], 0)
    twist = 2 * np.pi * ((source[:, None] + offset) * lane[None, :] % total) / total
    inner = 2 * np.pi * (lane[:, None] * lane[None, :] % width) / width
    cos, sin = np.cos(inner), np.sin(inner)
    forward = np.block([[cos, -sin], [sin, cos]])
    backward = np.block([[cos, sin], [-sin, cos]])
    finish = np.concatenate([np.cos(start_angle.T), -np.sin(start_angle.T)], 1) / total
    narrow = [jnp.asarray(table, jnp.bfloat16) for table in (start, forward, backward, finish)]
    wide = [jnp.asarray(table, jnp.float32) for table in (np.cos(twist), np.sin(twist))]
    return (*narrow, *wide)


def dot(left, right):
    return jnp.dot(left, right, preferred_element_type=jnp.float32)


def forward_spectrum(signal, spectrum, mixed, tables):
    start, forward, _, _, twist_cos, twist_sin = tables
    blocks, chans, width = signal.shape

    def body(step, carry):
        first = pl.multiple_of(step * GROUP, GROUP)
        columns = signal[:, pl.ds(first, GROUP), :].astype(jnp.float32)
        columns = jnp.swapaxes(columns, 0, 1).astype(jnp.bfloat16)
        cos, sin = twist_cos[...], twist_sin[...]
        for chan in range(GROUP):
            stage = dot(start[...], columns[chan])
            real, imag = stage[:blocks], stage[blocks:]
            rows = slice(chan * blocks, (chan + 1) * blocks)
            mixed[rows, :width] = (real * cos + imag * sin).astype(jnp.bfloat16)
            mixed[rows, width:] = (imag * cos - real * sin).astype(jnp.bfloat16)
        spectrum[pl.ds(first * blocks, GROUP * blocks), :] = dot(mixed[...], forward[...])
        return carry

    lax.fori_loop(0, chans // GROUP, body, 0)


def inverse_product(left, right, conjugate, result, mixed, partial, columns, tables):
    _, _, backward, finish, twist_cos, twist_sin = tables
    blocks, chans, width = result.shape

    def body(step, carry):
        first = pl.multiple_of(step * GROUP, GROUP)
        rows = pl.ds(first * blocks, GROUP * blocks)
        left_real, left_imag = left[rows, :width], left[rows, width:]
        right_real, right_imag = right[rows, :width], right[rows, width:]
        if conjugate:
            real = left_real * right_real + left_imag * right_imag
            imag = left_real * right_imag - left_imag * right_real
        else:
            real = left_real * right_real - left_imag * right_imag
            imag = left_real * right_imag + left_imag * right_real
        mixed[:, :width] = real.astype(jnp.bfloat16)
        mixed[:, width:] = imag.astype(jnp.bfloat16)
        partial[...] = dot(mixed[...], backward[...])
        cos, sin = twist_cos[...], twist_sin[...]
        for chan in range(GROUP):
            here = slice(chan * blocks, (chan + 1) * blocks)
            real, imag = partial[here, :width], partial[here, width:]
            turned = jnp.concatenate([real * cos - imag * sin, real * sin + imag * cos], 0)
            columns[chan] = dot(finish[...], turned.astype(jnp.bfloat16))
        result[:, pl.ds(first, GROUP), :] = jnp.swapaxes(columns[...], 0, 1).astype(result.dtype)
        return carry

    lax.fori_loop(0, chans // GROUP, body, 0)


def scatter(source, target, send_sem, recv_sem, me, nseq, first=0, last=None):
    def body(shift, carry):
        peer = lax.rem(me + shift, nseq)
        pltpu.make_async_remote_copy(
            src_ref=source.at[peer],
            dst_ref=target.at[me],
            send_sem=send_sem,
            recv_sem=recv_sem,
            device_id={"seq": peer},
            device_id_type=MESH,
        ).start()
        return carry

    lax.fori_loop(max(first, 1), nseq if last is None else last, body, 0)
    if first == 0:
        pltpu.make_async_copy(source.at[me], target.at[me], recv_sem).start()


def take(ref, sem):
    pltpu.make_async_copy(ref, ref, sem).wait()


def times(left, right, result):
    def body(step, carry):
        rows = pl.ds(step * 8, 8)
        product = left[rows].astype(jnp.float32) * right[rows].astype(jnp.float32)
        result[rows] = product.astype(result.dtype)
        return carry

    lax.fori_loop(0, left.shape[0] // 8, body, 0)


def kernel(
    factor,
    grad_out,
    gate,
    value,
    taps,
    start_far,
    forward_far,
    backward_far,
    finish_far,
    twist_cos_far,
    twist_sin_far,
    grad_gate,
    grad_back,
    filter_grad,
    grad_held,
    gate_held,
    gated,
    value_cols,
    gated_cols,
    taps_cols,
    conv_send,
    conv_back,
    grad_send,
    cross,
    y_send,
    y_recv,
    z_send,
    z_recv,
    spec_value,
    spec_gated,
    spec_taps,
    mixed,
    partial,
    columns,
    gate_out,
    filter_out,
    start,
    forward,
    backward,
    finish,
    twist_cos,
    twist_sin,
    send_sem,
    recv_sem,
    load_sem,
):
    tables = (start, forward, backward, finish, twist_cos, twist_sin)
    nseq = value.shape[0]
    me = lax.axis_index("seq")
    dp = lax.axis_index("dp")
    plane, half = dp // 2, lax.rem(dp, 2)
    depth = lax.rem(me // 2, 4)
    upper = lax.rem(me // 8, 2)
    other_half = plane * 2 + 1 - half
    mine = lax.rem(plane + 4 - depth, 4)

    def taps_peer(step):
        far = lax.rem(step // 2, 2)
        peer = (step // 2) * 8 + mine * 2 + lax.rem(step, 2)
        return peer, plane * 2 + lax.rem(half + upper + far, 2)

    barrier = pltpu.get_barrier_semaphore()

    def greet(shift, carry):
        pl.semaphore_signal(
            barrier, inc=1, device_id={"seq": lax.rem(me + shift, nseq)}, device_id_type=MESH
        )
        return carry

    def greet_taps(step, carry):
        peer, row = taps_peer(step)

        @pl.when(row != dp)
        def _():
            pl.semaphore_signal(
                barrier, inc=1, device_id={"dp": row, "seq": peer}, device_id_type=MESH
            )

        return carry

    lax.fori_loop(1, nseq, greet, 0)
    lax.fori_loop(0, nseq // 4, greet_taps, 0)
    for shift in range(1, 4):
        neighbour = lax.rem(plane + shift, 4) * 2 + half
        pl.semaphore_signal(barrier, inc=1, device_id={"dp": neighbour}, device_id_type=MESH)
    pl.semaphore_signal(barrier, inc=1, device_id={"dp": other_half}, device_id_type=MESH)

    loads = [
        pltpu.make_async_copy(grad_out, grad_held, load_sem.at[0]),
        pltpu.make_async_copy(gate, gate_held, load_sem.at[1]),
    ]
    distant = (start_far, forward_far, backward_far, finish_far, twist_cos_far, twist_sin_far)
    fetches = [
        pltpu.make_async_copy(far, near, load_sem.at[4 + index])
        for index, (far, near) in enumerate(zip(distant, tables))
    ]
    for load in loads + fetches:
        load.start()
    for load in loads:
        load.wait()
    times(grad_held, gate_held, gated)
    pl.semaphore_wait(barrier, nseq + 3 + nseq // 8)

    scatter(value, value_cols, send_sem.at[1], recv_sem.at[1], me, nseq, 0, EARLY)
    scatter(value, value_cols, send_sem.at[1], recv_sem.at[8], me, nseq, EARLY)

    def send_taps(step, carry):
        peer, row = taps_peer(step)
        itself = jnp.logical_and(peer == me, row == dp)

        @pl.when(jnp.logical_not(itself))
        def _():
            pltpu.make_async_remote_copy(
                src_ref=taps.at[peer // 8, lax.rem(peer // 2, 4), lax.rem(peer, 2)],
                dst_ref=taps_cols.at[me // 8, depth, lax.rem(me, 2)],
                send_sem=send_sem.at[0],
                recv_sem=recv_sem.at[0],
                device_id={"dp": row, "seq": peer},
                device_id_type=MESH,
            ).start()

        @pl.when(itself)
        def _():
            pltpu.make_async_copy(
                taps.at[me // 8, depth, lax.rem(me, 2)],
                taps_cols.at[me // 8, depth, lax.rem(me, 2)],
                recv_sem.at[0],
            ).start()

        return carry

    lax.fori_loop(0, nseq // 4, send_taps, 0)
    take(value_cols.at[pl.ds(0, EARLY)], recv_sem.at[1])
    scatter(gated, gated_cols, send_sem.at[2], recv_sem.at[2], me, nseq)

    for fetch in fetches:
        fetch.wait()
    take(taps_cols.at[:, mine], recv_sem.at[0])
    for shift in range(1, 4):
        neighbour = lax.rem(plane + shift, 4) * 2 + half
        pltpu.make_async_remote_copy(
            src_ref=taps_cols.at[:, mine],
            dst_ref=taps_cols.at[:, mine],
            send_sem=send_sem.at[3],
            recv_sem=recv_sem.at[3],
            device_id={"dp": neighbour},
            device_id_type=MESH,
        ).start()
    take(taps_cols.at[:, pl.ds(0, 3)], recv_sem.at[3])
    forward_spectrum(taps_cols.reshape(value.shape), spec_taps, mixed, tables)

    take(value_cols.at[pl.ds(EARLY, nseq - EARLY)], recv_sem.at[8])
    forward_spectrum(value_cols, spec_value, mixed, tables)
    inverse_product(spec_taps, spec_value, False, conv_send, mixed, partial, columns, tables)
    scatter(conv_send, conv_back, send_sem.at[4], recv_sem.at[4], me, nseq, 0, FIRST)

    take(gated_cols, recv_sem.at[2])
    forward_spectrum(gated_cols, spec_gated, mixed, tables)
    inverse_product(spec_value, spec_gated, True, cross, mixed, partial, columns, tables)
    for shift in range(1, 4):
        other = lax.rem(plane + shift, 4)
        y_send[shift - 1] = cross[pl.ds(other * 16, 16)].astype(y_send.dtype)
    for shift in range(1, 4):
        other = lax.rem(plane + shift, 4)
        pltpu.make_async_remote_copy(
            src_ref=y_send.at[shift - 1],
            dst_ref=y_recv.at[shift - 1],
            send_sem=send_sem.at[6],
            recv_sem=recv_sem.at[6],
            device_id={"dp": other * 2 + half},
            device_id_type=MESH,
        ).start()
    scatter(conv_send, conv_back, send_sem.at[4], recv_sem.at[4], me, nseq, FIRST)
    inverse_product(spec_taps, spec_gated, True, grad_send, mixed, partial, columns, tables)
    scatter(grad_send, grad_back, send_sem.at[5], recv_sem.at[5], me, nseq, 0, HALF)

    take(y_recv, recv_sem.at[6])

    def plane_sum(part):
        rows = pl.ds(8 * part, 8)
        terms = [y_recv[index, rows].astype(jnp.float32) for index in range(3)]
        return cross[pl.ds(plane * 16 + 8 * part, 8)] + terms[0] + terms[1] + terms[2]

    z_send[...] = plane_sum(1 - half).astype(z_send.dtype)
    swap = pltpu.make_async_remote_copy(
        src_ref=z_send,
        dst_ref=z_recv,
        send_sem=send_sem.at[7],
        recv_sem=recv_sem.at[7],
        device_id={"dp": other_half},
        device_id_type=MESH,
    )
    swap.start()
    scatter(grad_send, grad_back, send_sem.at[5], recv_sem.at[5], me, nseq, HALF)

    take(conv_back, recv_sem.at[4])
    times(grad_held, conv_back, gate_out)
    gate_store = pltpu.make_async_copy(gate_out, grad_gate, load_sem.at[2])
    gate_store.start()

    total = plane_sum(half)
    swap.wait()
    width = value.shape[2]
    total = (total + z_recv[...].astype(jnp.float32)) * factor
    for block in range(8):
        filter_out[:, block * width : (block + 1) * width] = total[block]
    filter_store = pltpu.make_async_copy(filter_out, filter_grad, load_sem.at[3])
    filter_store.start()
    gate_store.wait()

    for index, ref in ((1, value_cols), (2, gated), (4, conv_send)):
        take(ref.at[pl.ds(0, nseq - 1)], send_sem.at[index])
    take(taps_cols.at[:, pl.ds(0, 3)], send_sem.at[3])
    take(y_recv, send_sem.at[6])
    itself_too = mine == depth

    @pl.when(itself_too)
    def _():
        take(value_cols.at[pl.ds(0, nseq // 4 - 1)], send_sem.at[0])

    @pl.when(jnp.logical_not(itself_too))
    def _():
        take(value_cols.at[pl.ds(0, nseq // 4)], send_sem.at[0])

    take(grad_send.at[pl.ds(0, nseq - 1)], send_sem.at[5])
    filter_store.wait()
    take(grad_back, recv_sem.at[5])


def flush(*refs):
    count = len(refs) // 3
    sources, targets, held = refs[:count], refs[count : 2 * count], refs[2 * count : 3 * count]
    loads, stores = [], []
    for index in range(count):
        rows = held[index].shape[0] // 4
        for step in range(4):
            part = pl.ds(step * rows, rows)
            sem = 4 * index + step
            loads.append(
                pltpu.make_async_copy(
                    sources[index].at[part], held[index].at[part], refs[-1].at[0, sem]
                )
            )
            stores.append(
                pltpu.make_async_copy(
                    held[index].at[part], targets[index].at[part], refs[-1].at[1, sem]
                )
            )
    for load in loads:
        load.start()
    for load, store in zip(loads, stores):
        load.wait()
        store.start()
    for store in stores:
        store.wait()


def run_kernel(grad_out, gate, value, taps, factor):
    nseq, group, width = value.shape
    narrow, wide = jnp.bfloat16, jnp.float32
    blocks = (nseq, group, width)
    shapes = [
        jax.ShapeDtypeStruct(blocks, narrow),
        jax.ShapeDtypeStruct(blocks, narrow),
        jax.ShapeDtypeStruct((group, nseq * width // 8), wide),
    ]
    tables = make_tables(nseq, width)
    quarters = (nseq // 8, 4, 2, group, width)
    spec = (group * nseq, 2 * width)
    part = (GROUP * nseq, 2 * width)
    far = pl.BlockSpec(memory_space=pl.ANY)
    results = pl.pallas_call(
        functools.partial(kernel, factor),
        out_shape=shapes,
        in_specs=[far] * (4 + len(tables)),
        out_specs=[far] * 3,
        scratch_shapes=[pltpu.VMEM(blocks, narrow) for _ in range(5)]
        + [pltpu.VMEM(quarters, narrow)]
        + [pltpu.VMEM(blocks, narrow) for _ in range(3)]
        + [
            pltpu.VMEM(blocks, wide),
            pltpu.VMEM((3, 16, group, width), narrow),
            pltpu.VMEM((3, 16, group, width), narrow),
            pltpu.VMEM((8, group, width), narrow),
            pltpu.VMEM((8, group, width), narrow),
            pltpu.VMEM(spec, wide),
            pltpu.VMEM(spec, wide),
            pltpu.VMEM(spec, wide),
            pltpu.VMEM(part, narrow),
            pltpu.VMEM(part, wide),
            pltpu.VMEM((GROUP, nseq, width), wide),
            pltpu.VMEM(blocks, narrow),
            pltpu.VMEM((group, nseq * width // 8), wide),
        ]
        + [pltpu.VMEM(table.shape, table.dtype) for table in tables]
        + [
            pltpu.SemaphoreType.DMA((8,)),
            pltpu.SemaphoreType.DMA((9,)),
            pltpu.SemaphoreType.DMA((10,)),
        ],
        compiler_params=pltpu.CompilerParams(
            collective_id=0, has_side_effects=True, vmem_limit_bytes=60 * 2**20
        ),
    )(grad_out, gate, value, taps.reshape(quarters), *tables)
    return pl.pallas_call(
        flush,
        out_shape=shapes,
        in_specs=[far] * 3,
        out_specs=[far] * 3,
        scratch_shapes=[pltpu.VMEM(shape.shape, shape.dtype) for shape in shapes]
        + [pltpu.SemaphoreType.DMA((2, 12))],
        compiler_params=pltpu.CompilerParams(vmem_limit_bytes=60 * 2**20),
    )(*results)


def on_device(grad_out, gate, value, filter_taps):
    nseq = lax.axis_size("seq")
    ndp = lax.axis_size("dp")
    chans, width = grad_out.shape[1:]
    blocks = (nseq, chans // nseq, width)
    factor = 1.0 / (ndp * math.sqrt(nseq * width))
    grad_gate, grad_value, grad_filter = run_kernel(
        *(array.reshape(blocks) for array in (grad_out, gate, value, filter_taps)), factor
    )
    whole = (1, chans, width)
    return (grad_gate.reshape(whole), grad_value.reshape(whole), grad_filter)


def solution(mesh):
    return jax.shard_map(
        on_device,
        mesh=mesh,
        in_specs=(P("dp", None, "seq"), P("dp", None, "seq"), P("dp", None, "seq"), P(None, "seq")),
        out_specs=(P("dp", None, "seq"), P("dp", None, "seq"), P("seq", "dp")),
        check_vma=False,
    )
```

```python
import functools
import math

import jax
import jax.numpy as jnp
import numpy as np
from jax import lax
from jax.experimental import pallas as pl
from jax.experimental.pallas import tpu as pltpu
from jax.sharding import PartitionSpec as P

MESH = pl.DeviceIdType.MESH
GROUP = 16
EARLY = 40
FIRST = 46
HALF = 40


def make_tables(blocks, width, offset=0.25):
    total = blocks * width
    source = np.arange(blocks)
    lane = np.arange(width)
    start_angle = 2 * np.pi * ((source[:, None] + offset) * source[None, :] % blocks) / blocks
    start = np.concatenate([np.cos(start_angle), -np.sin(start_angle)], 0)
    twist = 2 * np.pi * ((source[:, None] + offset) * lane[None, :] % total) / total
    inner = 2 * np.pi * (lane[:, None] * lane[None, :] % width) / width
    cos, sin = np.cos(inner), np.sin(inner)
    forward = np.block([[cos, -sin], [sin, cos]])
    backward = np.block([[cos, sin], [-sin, cos]])
    finish = np.concatenate([np.cos(start_angle.T), -np.sin(start_angle.T)], 1) / total
    narrow = [jnp.asarray(table, jnp.bfloat16) for table in (start, forward, backward, finish)]
    wide = [jnp.asarray(table, jnp.float32) for table in (np.cos(twist), np.sin(twist))]
    return (*narrow, *wide)


def dot(left, right):
    return jnp.dot(left, right, preferred_element_type=jnp.float32)


def forward_spectrum(signal, spectrum, mixed, tables):
    start, forward, _, _, twist_cos, twist_sin = tables
    blocks, chans, width = signal.shape

    def body(step, carry):
        first = pl.multiple_of(step * GROUP, GROUP)
        columns = signal[:, pl.ds(first, GROUP), :].astype(jnp.float32)
        columns = jnp.swapaxes(columns, 0, 1).astype(jnp.bfloat16)
        cos, sin = twist_cos[...], twist_sin[...]
        for chan in range(GROUP):
            stage = dot(start[...], columns[chan])
            real, imag = stage[:blocks], stage[blocks:]
            rows = slice(chan * blocks, (chan + 1) * blocks)
            mixed[rows, :width] = (real * cos + imag * sin).astype(jnp.bfloat16)
            mixed[rows, width:] = (imag * cos - real * sin).astype(jnp.bfloat16)
        spectrum[pl.ds(first * blocks, GROUP * blocks), :] = dot(mixed[...], forward[...])
        return carry

    lax.fori_loop(0, chans // GROUP, body, 0)


def inverse_product(left, right, conjugate, result, mixed, partial, columns, tables):
    _, _, backward, finish, twist_cos, twist_sin = tables
    blocks, chans, width = result.shape

    def body(step, carry):
        first = pl.multiple_of(step * GROUP, GROUP)
        rows = pl.ds(first * blocks, GROUP * blocks)
        left_real, left_imag = left[rows, :width], left[rows, width:]
        right_real, right_imag = right[rows, :width], right[rows, width:]
        if conjugate:
            real = left_real * right_real + left_imag * right_imag
            imag = left_real * right_imag - left_imag * right_real
        else:
            real = left_real * right_real - left_imag * right_imag
            imag = left_real * right_imag + left_imag * right_real
        mixed[:, :width] = real.astype(jnp.bfloat16)
        mixed[:, width:] = imag.astype(jnp.bfloat16)
        partial[...] = dot(mixed[...], backward[...])
        cos, sin = twist_cos[...], twist_sin[...]
        for chan in range(GROUP):
            here = slice(chan * blocks, (chan + 1) * blocks)
            real, imag = partial[here, :width], partial[here, width:]
            turned = jnp.concatenate([real * cos - imag * sin, real * sin + imag * cos], 0)
            columns[chan] = dot(finish[...], turned.astype(jnp.bfloat16))
        result[:, pl.ds(first, GROUP), :] = jnp.swapaxes(columns[...], 0, 1).astype(result.dtype)
        return carry

    lax.fori_loop(0, chans // GROUP, body, 0)


def scatter(source, target, send_sem, recv_sem, me, nseq, first=0, last=None):
    def body(shift, carry):
        peer = lax.rem(me + shift, nseq)
        pltpu.make_async_remote_copy(
            src_ref=source.at[peer],
            dst_ref=target.at[me],
            send_sem=send_sem,
            recv_sem=recv_sem,
            device_id={"seq": peer},
            device_id_type=MESH,
        ).start()
        return carry

    lax.fori_loop(max(first, 1), nseq if last is None else last, body, 0)
    if first == 0:
        pltpu.make_async_copy(source.at[me], target.at[me], recv_sem).start()


def take(ref, sem):
    pltpu.make_async_copy(ref, ref, sem).wait()


def times(left, right, result):
    def body(step, carry):
        rows = pl.ds(step * 8, 8)
        product = left[rows].astype(jnp.float32) * right[rows].astype(jnp.float32)
        result[rows] = product.astype(result.dtype)
        return carry

    lax.fori_loop(0, left.shape[0] // 8, body, 0)


def kernel(
    factor,
    grad_out,
    gate,
    value,
    taps,
    start_far,
    forward_far,
    backward_far,
    finish_far,
    twist_cos_far,
    twist_sin_far,
    grad_gate,
    grad_back,
    filter_grad,
    grad_held,
    gate_held,
    gated,
    value_cols,
    gated_cols,
    taps_cols,
    conv_send,
    conv_back,
    grad_send,
    cross,
    y_send,
    y_recv,
    z_send,
    z_recv,
    spec_value,
    spec_gated,
    spec_taps,
    mixed,
    partial,
    columns,
    gate_out,
    filter_out,
    start,
    forward,
    backward,
    finish,
    twist_cos,
    twist_sin,
    send_sem,
    recv_sem,
    load_sem,
):
    tables = (start, forward, backward, finish, twist_cos, twist_sin)
    nseq = value.shape[0]
    me = lax.axis_index("seq")
    dp = lax.axis_index("dp")
    plane, half = dp // 2, lax.rem(dp, 2)
    depth = lax.rem(me // 2, 4)
    upper = lax.rem(me // 8, 2)
    other_half = plane * 2 + 1 - half
    mine = lax.rem(plane + 4 - depth, 4)

    def taps_peer(step):
        far = lax.rem(step // 2, 2)
        peer = (step // 2) * 8 + mine * 2 + lax.rem(step, 2)
        return peer, plane * 2 + lax.rem(half + upper + far, 2)

    barrier = pltpu.get_barrier_semaphore()

    def greet(shift, carry):
        pl.semaphore_signal(
            barrier, inc=1, device_id={"seq": lax.rem(me + shift, nseq)}, device_id_type=MESH
        )
        return carry

    def greet_taps(step, carry):
        peer, row = taps_peer(step)

        @pl.when(row != dp)
        def _():
            pl.semaphore_signal(
                barrier, inc=1, device_id={"dp": row, "seq": peer}, device_id_type=MESH
            )

        return carry

    lax.fori_loop(1, nseq, greet, 0)
    lax.fori_loop(0, nseq // 4, greet_taps, 0)
    for shift in range(1, 4):
        neighbour = lax.rem(plane + shift, 4) * 2 + half
        pl.semaphore_signal(barrier, inc=1, device_id={"dp": neighbour}, device_id_type=MESH)
    pl.semaphore_signal(barrier, inc=1, device_id={"dp": other_half}, device_id_type=MESH)

    loads = [
        pltpu.make_async_copy(grad_out, grad_held, load_sem.at[0]),
        pltpu.make_async_copy(gate, gate_held, load_sem.at[1]),
    ]
    distant = (start_far, forward_far, backward_far, finish_far, twist_cos_far, twist_sin_far)
    fetches = [
        pltpu.make_async_copy(far, near, load_sem.at[4 + index])
        for index, (far, near) in enumerate(zip(distant, tables))
    ]
    for load in loads + fetches:
        load.start()
    for load in loads:
        load.wait()
    times(grad_held, gate_held, gated)
    pl.semaphore_wait(barrier, nseq + 3 + nseq // 8)


    def send_taps(step, carry):
        peer, row = taps_peer(step)
        itself = jnp.logical_and(peer == me, row == dp)

        @pl.when(jnp.logical_not(itself))
        def _():
            pltpu.make_async_remote_copy(
                src_ref=taps.at[peer // 8, lax.rem(peer // 2, 4), lax.rem(peer, 2)],
                dst_ref=taps_cols.at[me // 8, depth, lax.rem(me, 2)],
                send_sem=send_sem.at[0],
                recv_sem=recv_sem.at[0],
                device_id={"dp": row, "seq": peer},
                device_id_type=MESH,
            ).start()

        @pl.when(itself)
        def _():
            pltpu.make_async_copy(
                taps.at[me // 8, depth, lax.rem(me, 2)],
                taps_cols.at[me // 8, depth, lax.rem(me, 2)],
                recv_sem.at[0],
            ).start()

        return carry

    lax.fori_loop(0, nseq // 4, send_taps, 0)
    scatter(value, value_cols, send_sem.at[1], recv_sem.at[1], me, nseq, 0, EARLY)
    take(taps_cols.at[:, mine], recv_sem.at[0])
    for shift in range(1, 4):
        neighbour = lax.rem(plane + shift, 4) * 2 + half
        pltpu.make_async_remote_copy(
            src_ref=taps_cols.at[:, mine],
            dst_ref=taps_cols.at[:, mine],
            send_sem=send_sem.at[3],
            recv_sem=recv_sem.at[3],
            device_id={"dp": neighbour},
            device_id_type=MESH,
        ).start()
    scatter(value, value_cols, send_sem.at[1], recv_sem.at[8], me, nseq, EARLY)
    take(value_cols.at[pl.ds(0, EARLY)], recv_sem.at[1])
    scatter(gated, gated_cols, send_sem.at[2], recv_sem.at[2], me, nseq)

    for fetch in fetches:
        fetch.wait()
    take(taps_cols.at[:, pl.ds(0, 3)], recv_sem.at[3])
    forward_spectrum(taps_cols.reshape(value.shape), spec_taps, mixed, tables)

    take(value_cols.at[pl.ds(EARLY, nseq - EARLY)], recv_sem.at[8])
    forward_spectrum(value_cols, spec_value, mixed, tables)
    inverse_product(spec_taps, spec_value, False, conv_send, mixed, partial, columns, tables)
    scatter(conv_send, conv_back, send_sem.at[4], recv_sem.at[4], me, nseq, 0, FIRST)

    take(gated_cols, recv_sem.at[2])
    forward_spectrum(gated_cols, spec_gated, mixed, tables)
    inverse_product(spec_value, spec_gated, True, cross, mixed, partial, columns, tables)
    for shift in range(1, 4):
        other = lax.rem(plane + shift, 4)
        y_send[shift - 1] = cross[pl.ds(other * 16, 16)].astype(y_send.dtype)
    for shift in range(1, 4):
        other = lax.rem(plane + shift, 4)
        pltpu.make_async_remote_copy(
            src_ref=y_send.at[shift - 1],
            dst_ref=y_recv.at[shift - 1],
            send_sem=send_sem.at[6],
            recv_sem=recv_sem.at[6],
            device_id={"dp": other * 2 + half},
            device_id_type=MESH,
        ).start()
    scatter(conv_send, conv_back, send_sem.at[4], recv_sem.at[4], me, nseq, FIRST)
    inverse_product(spec_taps, spec_gated, True, grad_send, mixed, partial, columns, tables)
    scatter(grad_send, grad_back, send_sem.at[5], recv_sem.at[5], me, nseq, 0, HALF)

    take(y_recv, recv_sem.at[6])

    def plane_sum(part):
        rows = pl.ds(8 * part, 8)
        terms = [y_recv[index, rows].astype(jnp.float32) for index in range(3)]
        return cross[pl.ds(plane * 16 + 8 * part, 8)] + terms[0] + terms[1] + terms[2]

    z_send[...] = plane_sum(1 - half).astype(z_send.dtype)
    swap = pltpu.make_async_remote_copy(
        src_ref=z_send,
        dst_ref=z_recv,
        send_sem=send_sem.at[7],
        recv_sem=recv_sem.at[7],
        device_id={"dp": other_half},
        device_id_type=MESH,
    )
    swap.start()
    scatter(grad_send, grad_back, send_sem.at[5], recv_sem.at[5], me, nseq, HALF)

    take(conv_back, recv_sem.at[4])
    times(grad_held, conv_back, gate_out)
    gate_store = pltpu.make_async_copy(gate_out, grad_gate, load_sem.at[2])
    gate_store.start()

    total = plane_sum(half)
    swap.wait()
    width = value.shape[2]
    total = (total + z_recv[...].astype(jnp.float32)) * factor
    for block in range(8):
        filter_out[:, block * width : (block + 1) * width] = total[block]
    filter_store = pltpu.make_async_copy(filter_out, filter_grad, load_sem.at[3])
    filter_store.start()
    gate_store.wait()

    for index, ref in ((1, value_cols), (2, gated), (4, conv_send)):
        take(ref.at[pl.ds(0, nseq - 1)], send_sem.at[index])
    take(taps_cols.at[:, pl.ds(0, 3)], send_sem.at[3])
    take(y_recv, send_sem.at[6])
    itself_too = mine == depth

    @pl.when(itself_too)
    def _():
        take(value_cols.at[pl.ds(0, nseq // 4 - 1)], send_sem.at[0])

    @pl.when(jnp.logical_not(itself_too))
    def _():
        take(value_cols.at[pl.ds(0, nseq // 4)], send_sem.at[0])

    take(grad_send.at[pl.ds(0, nseq - 1)], send_sem.at[5])
    filter_store.wait()
    take(grad_back, recv_sem.at[5])


def flush(*refs):
    count = len(refs) // 3
    sources, targets, held = refs[:count], refs[count : 2 * count], refs[2 * count : 3 * count]
    loads, stores = [], []
    for index in range(count):
        rows = held[index].shape[0] // 4
        for step in range(4):
            part = pl.ds(step * rows, rows)
            sem = 4 * index + step
            loads.append(
                pltpu.make_async_copy(
                    sources[index].at[part], held[index].at[part], refs[-1].at[0, sem]
                )
            )
            stores.append(
                pltpu.make_async_copy(
                    held[index].at[part], targets[index].at[part], refs[-1].at[1, sem]
                )
            )
    for load in loads:
        load.start()
    for load, store in zip(loads, stores):
        load.wait()
        store.start()
    for store in stores:
        store.wait()


def run_kernel(grad_out, gate, value, taps, factor):
    nseq, group, width = value.shape
    narrow, wide = jnp.bfloat16, jnp.float32
    blocks = (nseq, group, width)
    shapes = [
        jax.ShapeDtypeStruct(blocks, narrow),
        jax.ShapeDtypeStruct(blocks, narrow),
        jax.ShapeDtypeStruct((group, nseq * width // 8), wide),
    ]
    tables = make_tables(nseq, width)
    quarters = (nseq // 8, 4, 2, group, width)
    spec = (group * nseq, 2 * width)
    part = (GROUP * nseq, 2 * width)
    far = pl.BlockSpec(memory_space=pl.ANY)
    results = pl.pallas_call(
        functools.partial(kernel, factor),
        out_shape=shapes,
        in_specs=[far] * (4 + len(tables)),
        out_specs=[far] * 3,
        scratch_shapes=[pltpu.VMEM(blocks, narrow) for _ in range(5)]
        + [pltpu.VMEM(quarters, narrow)]
        + [pltpu.VMEM(blocks, narrow) for _ in range(3)]
        + [
            pltpu.VMEM(blocks, wide),
            pltpu.VMEM((3, 16, group, width), narrow),
            pltpu.VMEM((3, 16, group, width), narrow),
            pltpu.VMEM((8, group, width), narrow),
            pltpu.VMEM((8, group, width), narrow),
            pltpu.VMEM(spec, wide),
            pltpu.VMEM(spec, wide),
            pltpu.VMEM(spec, wide),
            pltpu.VMEM(part, narrow),
            pltpu.VMEM(part, wide),
            pltpu.VMEM((GROUP, nseq, width), wide),
            pltpu.VMEM(blocks, narrow),
            pltpu.VMEM((group, nseq * width // 8), wide),
        ]
        + [pltpu.VMEM(table.shape, table.dtype) for table in tables]
        + [
            pltpu.SemaphoreType.DMA((8,)),
            pltpu.SemaphoreType.DMA((9,)),
            pltpu.SemaphoreType.DMA((10,)),
        ],
        compiler_params=pltpu.CompilerParams(
            collective_id=0, has_side_effects=True, vmem_limit_bytes=60 * 2**20
        ),
    )(grad_out, gate, value, taps.reshape(quarters), *tables)
    return pl.pallas_call(
        flush,
        out_shape=shapes,
        in_specs=[far] * 3,
        out_specs=[far] * 3,
        scratch_shapes=[pltpu.VMEM(shape.shape, shape.dtype) for shape in shapes]
        + [pltpu.SemaphoreType.DMA((2, 12))],
        compiler_params=pltpu.CompilerParams(vmem_limit_bytes=60 * 2**20),
    )(*results)


def on_device(grad_out, gate, value, filter_taps):
    nseq = lax.axis_size("seq")
    ndp = lax.axis_size("dp")
    chans, width = grad_out.shape[1:]
    blocks = (nseq, chans // nseq, width)
    factor = 1.0 / (ndp * math.sqrt(nseq * width))
    grad_gate, grad_value, grad_filter = run_kernel(
        *(array.reshape(blocks) for array in (grad_out, gate, value, filter_taps)), factor
    )
    whole = (1, chans, width)
    return (grad_gate.reshape(whole), grad_value.reshape(whole), grad_filter)


def solution(mesh):
    return jax.shard_map(
        on_device,
        mesh=mesh,
        in_specs=(P("dp", None, "seq"), P("dp", None, "seq"), P("dp", None, "seq"), P(None, "seq")),
        out_specs=(P("dp", None, "seq"), P("dp", None, "seq"), P("seq", "dp")),
        check_vma=False,
    )
```
